32 devices in a mesh: dp: 8 (over z, core), mp: 4 (over y, x).
Axes of the slice: x: 2, y: 2, z: 4, core: 2. Of those that a mesh axis runs over, the one named last changes fastest.
Arguments:
- normed: bfloat16 [2048, 3072], P(('dp', 'mp')), may hold values from -6 to 6
- w_query: bfloat16 [3072, 1536], P(None, 'mp'), may hold values from -0.109375 to 0.109375
- query_gain: float32 [1536], P('mp'), may hold values from 0.1 to 1.9
- query_cot: bfloat16 [2048, 1536], P('dp', 'mp'), may hold values from -1.5 to 1.5
Outputs:
- queries: bfloat16 [2048, 1536], P('dp', 'mp')
- normed_grad: bfloat16 [2048, 3072], P(('dp', 'mp'))
- weight_grad: float32 [3072, 1536], P('dp', 'mp')
The draws below stay inside these ranges and needn't reach their ends.
All inputs are finite; a program needn't handle non-finite values.
Results may differ from the reference program's by a relative error of at most 0.018.
Values may be sent and summed in bfloat16 or wider, within the bound.
No kernel may reach another device: no remote copies, remote signals or barrier semaphores. Data moves between devices by JAX's collectives and lax.ppermute only.
A program may use at most 64 MiB of HBM per device.

```python
import jax
import jax.numpy as jnp
from jax import lax

D = 3072
HEAD = 128
TOK = 256
HD = 1536
TOKENS = 2048
N_DP = 8
N_MP = 4


def strengthened(entries, rng, source, target, parts, factor):
    owner, partner = [(jnp.arange(entries.shape[position]) // (entries.shape[position] // parts)).reshape([-1 if axis == position else 1 for axis in range(entries.ndim)]) for position in (source, target)]
    chosen = jax.random.permutation(rng, parts)[partner]
    strong = (owner == chosen) | (owner == (partner + parts // 2) % parts)
    return jnp.where(strong, factor * entries, entries)


def steps_of(key, shape, pieces, smallest, top_value):
    level, own = 1.0, jax.random.fold_in(key, 6)
    for dim, blocks in pieces:
        draws = jnp.exp(jax.random.uniform(jax.random.fold_in(own, dim), (blocks,), jnp.float32, smallest / len(pieces), top_value / len(pieces)))
        level = level * jnp.repeat(draws, shape[dim] // blocks).reshape([-1 if axis == dim else 1 for axis in range(len(shape))])
    return level


def noise(stream_key, dims, spread, most, cuts=(), held_as=jnp.bfloat16):
    array = spread * jax.random.normal(stream_key, dims, jnp.float32)
    if cuts:
        array = array * steps_of(stream_key, dims, cuts, -0.22, 0.18)
    return jnp.clip(array, -most, most).astype(held_as)


def gaussian_with(own_key, extent, spread, limit, cuts, heavy, held_as=jnp.bfloat16):
    result = spread * jax.random.normal(own_key, extent, jnp.float32)
    if cuts:
        result = result * steps_of(own_key, extent, cuts, -0.22, 0.18)
    return jnp.clip(strengthened(result, jax.random.fold_in(own_key, 3), *heavy), -limit, limit).astype(held_as)


def setup_inputs(seed: int = 0) -> dict:
    streams_of = jax.random.split(jax.random.key(seed), 5)
    normed = gaussian_with(streams_of[0], (TOKENS, D), 1.0, 6.0, ((0, 32),), (0, 1, 32, 2.75))
    w_query = noise(streams_of[1], (D, HD), D ** -0.5, 0.109375, ((1, 4),))
    query_gain = jnp.clip(1.0 + 0.18 * jax.random.normal(streams_of[2], (HD,), jnp.float32), 0.1, 1.9)
    query_cot = noise(streams_of[3], (TOKENS, HD), 0.25, 1.5, ((0, 8), (1, 4)))
    return {"normed": normed, "w_query": w_query, "query_gain": query_gain, "query_cot": query_cot}


def image_group(tokens_in, cot_in, w_query, query_gain):
    projected = jnp.dot(tokens_in, w_query, preferred_element_type=jnp.float32)
    tok_count = tokens_in.shape[0]
    heads_view = projected.reshape(tok_count, -1, HEAD)
    average = lax.optimization_barrier(jnp.mean(heads_view, axis=-1, keepdims=True))
    centred = heads_view - average
    spread_inv = lax.rsqrt(lax.optimization_barrier(jnp.mean(centred * centred, axis=-1, keepdims=True)) + 1e-06)
    unit = centred * spread_inv
    gain_view = query_gain.reshape(-1, HEAD)
    queries = (unit * gain_view).reshape(tok_count, -1).astype(jnp.bfloat16)
    scaled = cot_in.astype(jnp.float32).reshape(tok_count, -1, HEAD) * gain_view
    pre_grad = spread_inv * (scaled - lax.optimization_barrier(jnp.mean(scaled, axis=-1, keepdims=True)) - unit * lax.optimization_barrier(jnp.mean(scaled * unit, axis=-1, keepdims=True)))
    pre_grad = pre_grad.reshape(tok_count, -1).astype(jnp.bfloat16)
    grad_blocks = pre_grad.astype(jnp.float32).reshape(tok_count, N_MP, -1)
    weight_blocks = w_query.astype(jnp.float32).reshape(D, N_MP, -1)
    part_grad = jnp.einsum('tnc,dnc->ntd', grad_blocks, weight_blocks).astype(jnp.bfloat16)
    part_grad = lax.optimization_barrier(part_grad)
    normed_grad = lax.optimization_barrier(jnp.sum(part_grad.astype(jnp.float32), axis=0)).astype(jnp.bfloat16)
    group_grad = lax.dot_general(tokens_in, pre_grad, (((0,), (0,)), ((), ())), preferred_element_type=jnp.float32)
    return (queries, normed_grad, group_grad)

def reference(normed, w_query, query_gain, query_cot):
    token_groups = normed.reshape(N_DP, TOK, D)
    cot_groups = query_cot.reshape(N_DP, TOK, HD)

    def step_group(total, pair):
        queries, normed_grad, group_grad = image_group(pair[0], pair[1], w_query, query_gain)
        return (total + group_grad, (queries, normed_grad))
    weight_grad, outs = lax.scan(step_group, jnp.zeros((D, HD), jnp.float32), (token_groups, cot_groups))
    queries, normed_grad = outs
    return (queries.reshape(TOKENS, HD), normed_grad.reshape(TOKENS, D), weight_grad)
```

```python
import functools

import jax
import jax.numpy as jnp
from jax import lax
from jax.experimental import pallas as pl
from jax.experimental.pallas import tpu as pltpu
from jax.sharding import PartitionSpec as P

HEAD = 128
LANES = 128
PIECE_ROWS = 32
F32 = jnp.float32
BF16 = jnp.bfloat16


def call(body, out_shape, *operands, scratch=()):
    vmem = pl.BlockSpec(memory_space=pltpu.VMEM)
    return pl.pallas_call(
        body,
        out_shape=out_shape,
        in_specs=[vmem] * len(operands),
        out_specs=jax.tree.map(lambda _: vmem, out_shape),
        scratch_shapes=list(scratch),
        compiler_params=pltpu.CompilerParams(vmem_limit_bytes=48 << 20),
    )(*operands)


def exchange(value, axis, size, flip):
    return lax.ppermute(value, axis, [(i, i ^ flip) for i in range(size)])


def bits_of(k):
    return [1 << b for b in range(k.bit_length()) if k >> b & 1]


def rows_at(index, rows):
    return pl.ds(pl.multiple_of(index * rows, rows), rows)


def normalize(projected, gain, cot):
    queries, grads = [], []
    for h in range(0, projected.shape[1], HEAD):
        block = projected[:, h : h + HEAD]
        average = jnp.mean(block, axis=-1, keepdims=True)
        centred = block - average
        spread_inv = lax.rsqrt(jnp.mean(centred * centred, axis=-1, keepdims=True) + 1e-06)
        unit = centred * spread_inv
        head_gain = gain[:, h : h + HEAD]
        queries.append((unit * head_gain).astype(BF16))
        scaled = cot[:, h : h + HEAD].astype(F32) * head_gain
        grads.append(
            (
                spread_inv
                * (
                    scaled
                    - jnp.mean(scaled, axis=-1, keepdims=True)
                    - unit * jnp.mean(scaled * unit, axis=-1, keepdims=True)
                )
            ).astype(BF16)
        )
    return jnp.concatenate(queries, axis=1), jnp.concatenate(grads, axis=1)


def project_body(chunks, rows, n_pieces, n_done, *refs):
    pieces, (w, gain, cot), rest = refs[:n_pieces], refs[n_pieces : n_pieces + 3], refs[n_pieces + 3 :]
    done, outs = rest[: len(n_done)], rest[len(n_done) :]
    me = lax.axis_index("mp")
    tokens = jnp.concatenate([p[...] for p in pieces], axis=0)
    projected = jnp.dot(tokens, w[...], preferred_element_type=F32)
    cots = jnp.concatenate([cot[rows_at(me ^ k, rows), :] for k in chunks], axis=0)
    queries, grads = normalize(projected, gain[...], cots)
    outs[1][...] = grads
    if not n_done:
        outs[0][...] = queries
        return
    for i, k in enumerate(chunks):
        outs[0][rows_at(me ^ k, rows), :] = queries[i * rows : (i + 1) * rows]
    for ref, ks in zip(done, n_done):
        for i, k in enumerate(ks):
            outs[0][rows_at(me ^ k, rows), :] = ref[i * rows : (i + 1) * rows, :]


def project(chunks, pieces, w, gain, cot, done, last):
    rows = cot.shape[0] // lax.axis_size("mp")
    width = w.shape[1]
    n = len(chunks) * rows
    shape = lambda r: jax.ShapeDtypeStruct((r, width), BF16)
    body = functools.partial(project_body, chunks, rows, len(pieces), [ks for ks, _ in done] if last else [])
    return call(
        body,
        (shape(cot.shape[0] if last else n), shape(n)),
        *pieces,
        w,
        gain,
        cot,
        *([q for _, q in done] if last else []),
    )


def token_grad_body(takes, rows, n_pre, *refs):
    pres, w, outs = refs[:n_pre], refs[n_pre], refs[n_pre + 1 :]
    for (src, i), out in zip(takes, outs):
        out[...] = lax.dot_general(
            pres[src][i * rows : (i + 1) * rows, :], w[...], (((1,), (1,)), ((), ())), preferred_element_type=F32
        ).astype(out.dtype)


def token_grad(takes, types, pres, w, rows):
    body = functools.partial(token_grad_body, takes, rows, len(pres))
    return call(body, tuple(jax.ShapeDtypeStruct((rows, w.shape[0]), t) for t in types), *pres, w)


def weight_grad_body(flips, wide, n_tok, n_pre, *refs):
    toks, pres = refs[:n_tok], refs[n_tok : n_tok + n_pre]
    outs = refs[n_tok + n_pre : n_tok + n_pre + len(flips)]
    me = lax.axis_index("dp")
    grads = jnp.concatenate([p[...] for p in pres], axis=0)

    def product(columns):
        block = jnp.concatenate([t[:, columns] for t in toks], axis=0)
        return lax.dot_general(block, grads, (((0,), (0,)), ((), ())), preferred_element_type=F32)

    if wide % LANES == 0:
        for flip, out in zip(flips, outs):
            out[...] = product(rows_at(me ^ flip, wide)).astype(out.dtype)
        return
    whole = refs[-1]
    whole[...] = product(slice(None))
    for flip, out in zip(flips, outs):
        out[...] = whole[rows_at(me ^ flip, wide), :].astype(out.dtype)


def weight_grad_blocks(flips, types, toks, pres):
    deep, width = toks[0].shape[1], pres[0].shape[1]
    wide = deep // lax.axis_size("dp")
    shapes = tuple(jax.ShapeDtypeStruct((wide, width), t) for t in types)
    body = functools.partial(weight_grad_body, flips, wide, len(toks), len(pres))
    scratch = [] if wide % LANES == 0 else [pltpu.VMEM((deep, width), F32)]
    return call(body, shapes, *toks, *pres, scratch=scratch)


def add_body(*refs):
    *terms, out = refs
    total = terms[0][...].astype(F32)
    for term in terms[1:]:
        total += term[...].astype(F32)
    out[...] = total.astype(out.dtype)


def add(dtype, *terms):
    return call(add_body, jax.ShapeDtypeStruct(terms[0].shape, dtype), *terms)


def local(normed, w_query, query_gain, query_cot):
    n_mp, n_dp = lax.axis_size("mp"), lax.axis_size("dp")
    rows = normed.shape[0]
    gain = query_gain.reshape(1, -1)
    over_mp = lambda v, flip: exchange(v, "mp", n_mp, flip)
    over_dp = lambda v, flip: exchange(v, "dp", n_dp, flip)

    held = {0: [normed]}
    order = sorted(range(1, n_mp), key=lambda k: (len(bits_of(k)), k))
    for k in order:
        ways = bits_of(k)
        parts = len(ways) if rows % (len(ways) * PIECE_ROWS) == 0 else 1
        share = rows // parts
        pieces = []
        for i in range(parts):
            source = held[k ^ ways[i]]
            source = source[0] if len(source) == 1 else jnp.concatenate(source)
            pieces.append(over_mp(source[i * share : (i + 1) * share], ways[i]))
        held[k] = pieces
    near = [0] + [k for k in order if len(bits_of(k)) == 1]
    far = [k for k in order if len(bits_of(k)) > 1]

    near_toks = [p for k in near for p in held[k]]
    far_toks = [p for k in far for p in held[k]]
    q_near, pre_near = project(near, near_toks, w_query, gain, query_cot, [], False)
    queries, pre_far = project(far, far_toks, w_query, gain, query_cot, [(near, q_near)], True)
    pres = [pre_near, pre_far]

    toks = near_toks + far_toks
    both_toks = toks + [over_dp(t, 1) for t in toks]
    both_pres = pres + [over_dp(p, 1) for p in pres]

    flips = list(range(0, n_dp, 2))
    leaves = [f for f in flips if f & 2]
    leaves.sort(key=lambda f: -len(bits_of(f)))
    stays = [f for f in flips if not f & 2]
    first = weight_grad_blocks(leaves[:1], [BF16], both_toks, both_pres)
    arrived = {leaves[0] ^ 2: [over_dp(first[0], 2)]}
    others = leaves[1:] + stays
    blocks = weight_grad_blocks(others, [BF16] * (len(leaves) - 1) + [F32] * len(stays), both_toks, both_pres)
    blocks = dict(zip(others, blocks))
    for f in leaves[1:]:
        arrived.setdefault(f ^ 2, []).append(over_dp(blocks[f], 2))
    hop = 4
    while hop < n_dp:
        for f in sorted((f for f in stays if f & hop), key=lambda f: -len(bits_of(f))):
            arrived.setdefault(f ^ hop, []).append(over_dp(add(BF16, blocks[f], *arrived[f]), hop))
        stays = [f for f in stays if not f & hop]
        hop *= 2
    weight_grad = add(F32, blocks[0], *arrived[0])

    at = {k: (s, i) for s, ks in enumerate((near, far)) for i, k in enumerate(ks)}
    near_terms = token_grad([at[k] for k in near[1:]], [BF16] * (len(near) - 1), [pre_near], w_query, rows)
    terms = [over_mp(t, k) for t, k in zip(near_terms, near[1:])]
    far_terms = token_grad([at[k] for k in far] + [at[0]], [BF16] * len(far) + [F32], pres[::1], w_query, rows)
    terms += [over_mp(t, k) for t, k in zip(far_terms, far)]
    normed_grad = add(BF16, far_terms[-1], *terms)
    return queries, normed_grad, weight_grad


def solution(mesh):
    return jax.shard_map(
        local,
        mesh=mesh,
        in_specs=(P(("dp", "mp"), None), P(None, "mp"), P("mp"), P("dp", "mp")),
        out_specs=(P("dp", "mp"), P(("dp", "mp"), None), P("dp", "mp")),
        check_vma=False,
    )
```
